256 devices in a mesh: energy: 32 (over x, y, core), cell: 8 (over z).
Axes of the slice: x: 4, y: 4, z: 8, core: 2. Of those that a mesh axis runs over, the one named last changes fastest.
Arguments:
- retarded_diag: bfloat16 [2, 64, 32, 256, 256], P(None, 'energy', 'cell'), may hold values from -0.375 to 0.375
- retarded_lower: bfloat16 [2, 64, 32, 256, 256], P(None, 'energy', 'cell'), may hold values from -0.375 to 0.375
- retarded_upper: bfloat16 [2, 64, 32, 256, 256], P(None, 'energy', 'cell'), may hold values from -0.375 to 0.375
- sigma_lesser: bfloat16 [2, 64, 32, 256, 256], P(None, 'energy', 'cell'), may hold values from -6 to 6
- screened: bfloat16 [2, 32, 128], P(None, 'cell'), may hold values from -0.5 to 0.5
- kept: int32 [32, 8], P('cell'), may hold values from 0 to 15, as said below
- kept_count: int32 [32], P('cell'), may hold values from 1 to 8, as said below
Outputs:
- sigma_new: bfloat16 [2, 64, 32, 8, 4096], P(None, 'energy', 'cell')
The draws below stay inside these ranges and needn't reach their ends.
Inputs may be any that keep to these rules, and one draw needn't show every extreme that they name: `kept`: each row holds 8 different sub-block numbers. `kept_count`: some cell has 8 live slots and some other cell 1.
All inputs are finite; a program needn't handle non-finite values.
Results may differ from the reference program's by a relative error of at most 0.0057.
Values may be sent and summed in bfloat16 or wider, within the bound.
A program may use at most 128 MiB of HBM per device.

```python
import jax
import jax.numpy as jnp
from jax import lax

ORB = 256
SUB = 64
KMAX = 8
ENERGIES = 64
CELLS = 32


def draw_kept(key, part):
    block_count = ORB // SUB * (ORB // SUB)
    key_scores = jax.random.fold_in(key, 101)
    scores = jax.random.randint(key_scores, (CELLS, block_count), 0, 1 << 20) * block_count
    scores = scores + jnp.arange(block_count, dtype=jnp.int32)[None, :]
    return lax.top_k(scores, KMAX)[1].astype(jnp.int32)


def draw_kept_count(key, part):
    key_counts = jax.random.fold_in(key, 202)
    key_full = jax.random.fold_in(key, 303)
    key_empty = jax.random.fold_in(key, 404)
    counts = jax.random.randint(key_counts, (CELLS,), 1, KMAX + 1)
    fullest = jax.random.randint(key_full, (), 0, CELLS)
    emptiest = (fullest + 1 + jax.random.randint(key_empty, (), 0, CELLS - 1)) % CELLS
    position = jnp.arange(CELLS, dtype=jnp.int32)
    counts = jnp.where(position == emptiest, 1, counts)
    counts = jnp.where(position == fullest, KMAX, counts)
    return counts.astype(jnp.int32)


def level_of(key, dims, pieces, smallest, top_value):
    def one(dim, blocks):
        heights = jax.random.uniform(jax.random.fold_in(jax.random.fold_in(key, 6), dim), (blocks,), jnp.float32, smallest / len(pieces), top_value / len(pieces))
        return jnp.repeat(jnp.exp(heights), dims[dim] // blocks).reshape((-1,) + (1,) * (len(dims) - dim - 1))

    factor_of = one(*pieces[0])
    for cut in pieces[1:]:
        factor_of = factor_of * one(*cut)
    return factor_of


def scatter_about(own_key, shape, scale, limit, split=(), kind=jnp.bfloat16):
    factor_of = level_of(own_key, shape, split, -0.22, 0.18) if split else 1.0
    values = jax.random.normal(own_key, shape, jnp.float32) * scale * factor_of
    return jnp.minimum(jnp.maximum(values, -limit), limit).astype(kind)


def setup_inputs(seed: int = 0) -> dict:
    key_list = jax.random.split(jax.random.key(seed), 8)
    retarded_diag = scatter_about(key_list[0], (2, ENERGIES, CELLS, ORB, ORB), ORB ** -0.5, 0.375, ((1, 32), (2, 8)))
    retarded_lower = scatter_about(key_list[1], (2, ENERGIES, CELLS, ORB, ORB), ORB ** -0.5, 0.375, ((1, 32), (2, 8)))
    retarded_upper = scatter_about(key_list[2], (2, ENERGIES, CELLS, ORB, ORB), ORB ** -0.5, 0.375, ((1, 32), (2, 8)))
    sigma_lesser = scatter_about(key_list[3], (2, ENERGIES, CELLS, ORB, ORB), 1.0, 6.0, ((1, 32), (2, 8)))
    screened = scatter_about(key_list[4], (2, CELLS, 2 * ENERGIES), (2 * ENERGIES) ** -0.5, 0.5, ((1, 8),))
    kept = draw_kept(jax.random.fold_in(key_list[7], 71), 0)
    kept_count = draw_kept_count(jax.random.fold_in(key_list[7], 71), 0)
    return {"retarded_diag": retarded_diag, "retarded_lower": retarded_lower, "retarded_upper": retarded_upper, "sigma_lesser": sigma_lesser, "screened": screened, "kept": kept, "kept_count": kept_count}


def batched(left_side, right_side):
    return jnp.einsum("cij,cjk->cik", left_side.astype(jnp.float32), right_side.astype(jnp.float32))


def batched_t(left_side, right_side):
    return jnp.einsum("cij,ckj->cik", left_side.astype(jnp.float32), right_side.astype(jnp.float32))


def sandwich(factor, middle):
    inner_r = (batched(factor[0], middle[0]) - batched(factor[1], middle[1])).astype(jnp.bfloat16)
    inner_i = (batched(factor[0], middle[1]) + batched(factor[1], middle[0])).astype(jnp.bfloat16)
    outer_r = batched_t(inner_r, factor[0]) + batched_t(inner_i, factor[1])
    outer_i = batched_t(inner_i, factor[0]) - batched_t(inner_r, factor[1])
    return outer_r, outer_i


def lesser_one(inputs):
    retarded_diag, retarded_lower, retarded_upper, sigma_lesser = inputs
    zero_cell = jnp.zeros_like(sigma_lesser[:, :1])
    prev_cell = jnp.concatenate([zero_cell, sigma_lesser[:, :-1]], axis=1)
    next_cell = jnp.concatenate([sigma_lesser[:, 1:], zero_cell], axis=1)
    first_r, first_i = sandwich(retarded_diag, sigma_lesser)
    second_r, second_i = sandwich(retarded_lower, prev_cell)
    third_r, third_i = sandwich(retarded_upper, next_cell)
    real_part = first_r + second_r + third_r
    imag_part = first_i + second_i + third_i
    return jnp.stack([real_part, imag_part]).astype(jnp.bfloat16)


def select_blocks(blocks, kept, sub_size):
    per_side = blocks.shape[3]
    row_pick = (kept // per_side)[None, None, :, :, None, None]
    col_pick = (kept % per_side)[None, None, :, :, None, None, None]
    row_blocks = jnp.take_along_axis(blocks, row_pick, axis=3)
    shaped = row_blocks.reshape(row_blocks.shape[:5] + (per_side, sub_size))
    picked = jnp.take_along_axis(shaped, col_pick, axis=5)
    return picked.reshape(picked.shape[:4] + (picked.shape[4] * sub_size,))


def toeplitz(screened):
    energy_count = screened.shape[2] // 2
    position = jnp.arange(energy_count, dtype=jnp.int32)
    offsets = position[:, None] - position[None, :] + energy_count - 1
    return jnp.take(screened, offsets, axis=2)


def convolve(kernel, chosen):
    kernel_r = kernel[0].astype(jnp.float32)
    kernel_i = kernel[1].astype(jnp.float32)
    chosen_r = chosen[0].astype(jnp.float32)
    chosen_i = chosen[1].astype(jnp.float32)
    real_part = jnp.einsum("cef,fckn->eckn", kernel_r, chosen_r) - jnp.einsum("cef,fckn->eckn", kernel_i, chosen_i)
    imag_part = jnp.einsum("cef,fckn->eckn", kernel_r, chosen_i) + jnp.einsum("cef,fckn->eckn", kernel_i, chosen_r)
    return jnp.stack([real_part, imag_part]).astype(jnp.bfloat16)


def reference(retarded_diag, retarded_lower, retarded_upper, sigma_lesser, screened, kept, kept_count):
    inputs = tuple(jnp.moveaxis(item, 1, 0) for item in (retarded_diag, retarded_lower, retarded_upper, sigma_lesser))
    lesser = jnp.moveaxis(lax.map(lesser_one, inputs), 0, 1)
    per_side = ORB // SUB
    blocks = lesser.reshape(2, ENERGIES, CELLS, per_side, SUB, ORB)
    chosen = select_blocks(blocks, kept, SUB)
    live_slots = (jnp.arange(KMAX, dtype=jnp.int32)[None, :] < kept_count[:, None]).astype(jnp.bfloat16)
    chosen = chosen * live_slots[None, None, :, :, None]
    return convolve(toeplitz(screened), chosen)
```

```python
import jax
import jax.numpy as jnp
from jax import lax
from jax.experimental import pallas as pl
from jax.experimental.pallas import tpu as pltpu
from jax.sharding import PartitionSpec as P

ORB = 256
SUB = 64
KMAX = 8
LANES = 128
BF = jnp.bfloat16
F32 = jnp.float32


def mm(a, b):
    return jnp.dot(a, b, preferred_element_type=F32)


def mm_t(a, b):
    return lax.dot_general(a, b, (((1,), (1,)), ((), ())), preferred_element_type=F32)


def one_side(gr, gi, sr, si):
    inner_r = mm(jnp.concatenate([gr, -gi], 1), jnp.concatenate([sr, si], 0)).astype(BF)
    inner_i = mm(jnp.concatenate([gr, gi], 1), jnp.concatenate([si, sr], 0)).astype(BF)
    rows = []
    for b in range(ORB // SUB):
        part = slice(b * SUB, (b + 1) * SUB)
        rows.append(jnp.concatenate([gr[part], gi[part]], 1))
        rows.append(jnp.concatenate([-gi[part], gr[part]], 1))
    return mm_t(jnp.concatenate([inner_r, inner_i], 1), jnp.concatenate(rows, 0))


def lesser_cell(c, kept, count, g3, sx, l32, sel32, put):
    def energy(e, carry):
        total = one_side(g3[0][0, e, c], g3[0][1, e, c], sx[0, e, c + 1], sx[1, e, c + 1])
        total += one_side(g3[1][0, e, c], g3[1][1, e, c], sx[0, e, c], sx[1, e, c])
        total += one_side(g3[2][0, e, c], g3[2][1, e, c], sx[0, e, c + 2], sx[1, e, c + 2])
        for rb in range(ORB // SUB):
            for cb in range(ORB // SUB):
                l32[rb * 4 + cb] = total[rb * SUB : (rb + 1) * SUB, cb * LANES : (cb + 1) * LANES]
        live = count[c]
        for j in range(KMAX):
            sel32[j * 2 + e] = l32[kept[c, j]] * jnp.where(j < live, 1.0, 0.0).astype(F32)
        return carry

    lax.fori_loop(0, 2, energy, 0)
    low = lax.broadcasted_iota(jnp.int32, (16, LANES), 1) < SUB
    for d in range(32):
        even = sel32[:, 2 * d, :]
        odd = sel32[:, 2 * d + 1, :]
        put(d, 0, jnp.where(low, even, pltpu.roll(odd, SUB, 1)).astype(BF))
        put(d, 1, jnp.where(low, pltpu.roll(even, SUB, 1), odd).astype(BF))


def iota(shape, dim):
    return lax.broadcasted_iota(jnp.int32, shape, dim)


def build_kernels(screened, kmat):
    shape = (LANES, LANES)
    flip = (iota(shape, 0) == 126 - iota(shape, 1)).astype(BF)
    row, col = iota(shape, 0), iota(shape, 1)
    source = ((row // 2) % 2) * 64 + (row // 4) * 2 + row % 2
    row_pick = (source == col).astype(BF)
    wanted = (col // 64) * 64 + (col % 32) * 2 + (col // 32) % 2
    col_pick = (wanted == row).astype(BF)
    srow = iota((64, LANES), 0)
    low = iota((64, LANES), 1) < 64
    for c in range(4):
        halves = []
        for p in range(2):
            rev = mm(screened[p].astype(BF), flip)[c : c + 1]
            x = pltpu.roll(jnp.broadcast_to(rev, (64, LANES)), 65, 1)
            for bit in range(6):
                x = jnp.where((srow >> bit) % 2 == 1, pltpu.roll(x, 1 << bit, 1), x)
            halves.append(x)
        kr, ki = halves
        top = jnp.where(low, kr, pltpu.roll(-ki, 64, 1))
        bottom = jnp.where(low, ki, pltpu.roll(kr, 64, 1))
        natural = jnp.concatenate([top, bottom], 0).astype(BF)
        kmat[c] = mm(mm(row_pick, natural).astype(BF), col_pick).astype(BF)


def conv_cell(kc, get, x32, o32, put):
    x32[...] = get().astype(F32)
    for j in range(KMAX):
        parts = []
        for p in range(2):
            for e2 in range(2):
                parts.append(x32[:, p, 2 * j + e2, :].astype(BF))
        o32[:, j, :] = mm(kc, jnp.concatenate(parts, 0))
    put(o32[...].astype(BF))


def lesser_kernel(kept, count, gd, gl, gu, s, lo, hi, send, vd, vl, vu, sx, l32, sel32, sems):
    z = lax.axis_index("cell")
    last = lax.axis_size("cell") - 1
    copies = [
        pltpu.make_async_copy(gd, vd, sems.at[0]),
        pltpu.make_async_copy(gl, vl, sems.at[1]),
        pltpu.make_async_copy(gu, vu, sems.at[2]),
        pltpu.make_async_copy(s, sx.at[:, :, pl.ds(1, 4)], sems.at[3]),
        pltpu.make_async_copy(lo, sx.at[:, :, pl.ds(0, 1)], sems.at[4]),
        pltpu.make_async_copy(hi, sx.at[:, :, pl.ds(5, 1)], sems.at[5]),
    ]
    for copy in copies:
        copy.start()
    for copy in copies:
        copy.wait()

    def cell(c, carry):
        def put(d, p, value):
            send[d, c, p] = value

        lesser_cell(c, kept, count, (vd, vl, vu), sx, l32, sel32, put)
        return carry

    lax.fori_loop(0, 4, cell, 0)


def conv_kernel(screened, recv, send, kmat, x32, o32):
    build_kernels(screened, kmat)

    def cell(c, carry):
        def put(value):
            send[:, pl.ds(c, 1)] = value.reshape(32, 1, 4, KMAX, LANES)

        conv_cell(kmat[c], lambda: recv[:, c], x32, o32, put)
        return carry

    lax.fori_loop(0, 4, cell, 0)


def place_kernel(recv, out):
    def source(d, carry):
        for c in range(4):
            for pe in range(4):
                out[pe, c, :, pl.ds(pl.multiple_of(d * LANES, LANES), LANES)] = recv[d, c, pe]
        return carry

    lax.fori_loop(0, 32, source, 0)


VM = pl.BlockSpec(memory_space=pltpu.VMEM)
SM = pl.BlockSpec(memory_space=pltpu.SMEM)
ANY = pl.BlockSpec(memory_space=pl.ANY)


def per_device(gd, gl, gu, s, screened, kept, count):
    n = lax.axis_size("cell")
    lo = lax.ppermute(s[:, :, 3:4], "cell", [(i, i + 1) for i in range(n - 1)])
    hi = lax.ppermute(s[:, :, 0:1], "cell", [(i + 1, i) for i in range(n - 1)])
    limit = pltpu.CompilerParams(vmem_limit_bytes=60 * 1024 * 1024)
    big = pltpu.VMEM((2, 2, 4, ORB, ORB), BF)
    send = pl.pallas_call(
        lesser_kernel,
        out_shape=jax.ShapeDtypeStruct((32, 4, 2, 16, LANES), BF),
        in_specs=[SM, SM, ANY, ANY, ANY, ANY, ANY, ANY],
        out_specs=VM,
        scratch_shapes=[
            big,
            big,
            big,
            pltpu.VMEM((2, 2, 6, ORB, ORB), BF),
            pltpu.VMEM((16, SUB, LANES), F32),
            pltpu.VMEM((16, SUB, LANES), F32),
            pltpu.SemaphoreType.DMA((6,)),
        ],
        compiler_params=limit,
        name="lesser",
    )(kept, count, gd, gl, gu, s, lo, hi)
    recv = lax.all_to_all(send, "energy", split_axis=0, concat_axis=0, tiled=True)
    back = pl.pallas_call(
        conv_kernel,
        out_shape=jax.ShapeDtypeStruct((32, 4, 4, KMAX, LANES), BF),
        in_specs=[VM, VM],
        out_specs=VM,
        scratch_shapes=[
            pltpu.VMEM((4, LANES, LANES), BF),
            pltpu.VMEM((32, 2, 16, LANES), F32),
            pltpu.VMEM((LANES, KMAX, LANES), F32),
        ],
        compiler_params=limit,
        name="conv",
    )(screened, recv)
    got = lax.all_to_all(back, "energy", split_axis=0, concat_axis=0, tiled=True)
    out = pl.pallas_call(
        place_kernel,
        out_shape=jax.ShapeDtypeStruct((4, 4, KMAX, SUB * SUB), BF),
        in_specs=[VM],
        out_specs=VM,
        compiler_params=limit,
        name="place",
    )(got)
    return out.reshape(2, 2, 4, KMAX, SUB * SUB)


def solution(mesh):
    placed = P(None, "energy", "cell", None, None)
    return jax.shard_map(
        per_device,
        mesh=mesh,
        in_specs=(placed, placed, placed, placed, P(None, "cell", None), P("cell", None), P("cell")),
        out_specs=placed,
        check_vma=False,
    )
```

```python
import jax
import jax.numpy as jnp
from jax import lax
from jax.experimental import pallas as pl
from jax.experimental.pallas import tpu as pltpu
from jax.sharding import PartitionSpec as P

ORB = 256
SUB = 64
KMAX = 8
LANES = 128
BF = jnp.bfloat16
F32 = jnp.float32


def mm(a, b):
    return jnp.dot(a, b, preferred_element_type=F32)


def mm_t(a, b):
    return lax.dot_general(a, b, (((1,), (1,)), ((), ())), preferred_element_type=F32)


def one_side(gr, gi, sr, si):
    inner_r = mm(jnp.concatenate([gr, -gi], 1), jnp.concatenate([sr, si], 0)).astype(BF)
    inner_i = mm(jnp.concatenate([gr, gi], 1), jnp.concatenate([si, sr], 0)).astype(BF)
    rows = []
    for b in range(ORB // SUB):
        part = slice(b * SUB, (b + 1) * SUB)
        rows.append(jnp.concatenate([gr[part], gi[part]], 1))
        rows.append(jnp.concatenate([-gi[part], gr[part]], 1))
    return mm_t(jnp.concatenate([inner_r, inner_i], 1), jnp.concatenate(rows, 0))


def lesser_cell(c, kept, count, g3, sx, l32, sel32, put):
    def energy(e, carry):
        total = one_side(g3[0][0, e, c], g3[0][1, e, c], sx[0, e, c + 1], sx[1, e, c + 1])
        total += one_side(g3[1][0, e, c], g3[1][1, e, c], sx[0, e, c], sx[1, e, c])
        total += one_side(g3[2][0, e, c], g3[2][1, e, c], sx[0, e, c + 2], sx[1, e, c + 2])
        for rb in range(ORB // SUB):
            for cb in range(ORB // SUB):
                l32[rb * 4 + cb] = total[rb * SUB : (rb + 1) * SUB, cb * LANES : (cb + 1) * LANES]
        live = count[c]
        for j in range(KMAX):
            sel32[j * 2 + e] = l32[kept[c, j]] * jnp.where(j < live, 1.0, 0.0).astype(F32)
        return carry

    lax.fori_loop(0, 2, energy, 0)
    low = lax.broadcasted_iota(jnp.int32, (16, LANES), 1) < SUB
    for d in range(32):
        even = sel32[:, 2 * d, :]
        odd = sel32[:, 2 * d + 1, :]
        put(d, 0, jnp.where(low, even, pltpu.roll(odd, SUB, 1)).astype(BF))
        put(d, 1, jnp.where(low, pltpu.roll(even, SUB, 1), odd).astype(BF))


def iota(shape, dim):
    return lax.broadcasted_iota(jnp.int32, shape, dim)


def build_kernels(screened, kmat):
    shape = (LANES, LANES)
    flip = (iota(shape, 0) == 126 - iota(shape, 1)).astype(BF)
    row, col = iota(shape, 0), iota(shape, 1)
    source = ((row // 2) % 2) * 64 + (row // 4) * 2 + row % 2
    row_pick = (source == col).astype(BF)
    wanted = (col // 64) * 64 + (col % 32) * 2 + (col // 32) % 2
    col_pick = (wanted == row).astype(BF)
    srow = iota((64, LANES), 0)
    low = iota((64, LANES), 1) < 64
    for c in range(4):
        halves = []
        for p in range(2):
            rev = mm(screened[p].astype(BF), flip)[c : c + 1]
            x = pltpu.roll(jnp.broadcast_to(rev, (64, LANES)), 65, 1)
            for bit in range(6):
                x = jnp.where((srow >> bit) % 2 == 1, pltpu.roll(x, 1 << bit, 1), x)
            halves.append(x)
        kr, ki = halves
        top = jnp.where(low, kr, pltpu.roll(-ki, 64, 1))
        bottom = jnp.where(low, ki, pltpu.roll(kr, 64, 1))
        natural = jnp.concatenate([top, bottom], 0).astype(BF)
        kmat[c] = mm(mm(row_pick, natural).astype(BF), col_pick).astype(BF)


def conv_cell(kc, get, x32, o32, put):
    x32[...] = get().astype(F32)
    for j in range(KMAX):
        parts = []
        for p in range(2):
            for e2 in range(2):
                parts.append(x32[:, p, 2 * j + e2, :].astype(BF))
        o32[:, j, :] = mm(kc, jnp.concatenate(parts, 0))
    put(o32[...].astype(BF))


def whole(kept, count, screened, gd, gl, gu, s, out, vd, vl, vu, sx, l32, sel32, send_a, recv_a, kmat, x32, o32, send_b,
          in_sem, s_sem, halo_send, halo_recv, a_send, a_recv, b_send, b_recv):
    me = lax.axis_index("energy")
    z = lax.axis_index("cell")
    up = lax.rem(z + 1, 8)
    down = lax.rem(z + 7, 8)
    own = pltpu.make_async_copy(s, sx.at[:, :, pl.ds(1, 4)], s_sem)
    own.start()

    def inputs(c):
        here = pl.ds(c, 1)
        return [
            pltpu.make_async_copy(g.at[:, :, here], v.at[:, :, here], in_sem.at[c, k])
            for k, (g, v) in enumerate(((gd, vd), (gl, vl), (gu, vu)))
        ]

    for c in (1, 2, 0, 3):
        for copy in inputs(c):
            copy.start()

    barrier = pltpu.get_barrier_semaphore()

    def greet(k, carry):
        pl.semaphore_signal(barrier, 1, device_id=(lax.rem(me + k, 32), z), device_id_type=MESH)
        return carry

    lax.fori_loop(1, 32, greet, 0)
    pl.semaphore_signal(barrier, 1, device_id=(me, up), device_id_type=MESH)
    pl.semaphore_signal(barrier, 1, device_id=(me, down), device_id_type=MESH)
    pl.semaphore_wait(barrier, 33)

    halos = [
        pltpu.make_async_remote_copy(
            s.at[:, :, pl.ds(source, 1)], sx.at[:, :, pl.ds(target, 1)], halo_send.at[k], halo_recv.at[k],
            device_id=(me, where), device_id_type=MESH,
        )
        for k, (source, target, where) in enumerate(((3, 0, up), (0, 5, down)))
    ]
    for halo in halos:
        halo.start()
    own.wait()

    def lesser(c):
        for copy in inputs(c):
            copy.wait()

        def put(d, p, value):
            send_a[c, d, p] = value

        lesser_cell(c, kept, count, (vd, vl, vu), sx, l32, sel32, put)
        pltpu.make_async_copy(send_a.at[c, me], recv_a.at[c, me], a_recv.at[c]).start()

        def push(k, carry):
            to = lax.rem(me + k, 32)
            pltpu.make_async_remote_copy(
                send_a.at[c, to], recv_a.at[c, me], a_send.at[c], a_recv.at[c],
                device_id=(to, z), device_id_type=MESH,
            ).start()
            return carry

        lax.fori_loop(1, 32, push, 0)

    def convolve(c):
        pltpu.make_async_copy(recv_a.at[c], recv_a.at[c], a_recv.at[c]).wait()

        def put(value):
            send_b[c] = value.reshape(32, 4, KMAX, LANES)

        conv_cell(kmat[c], lambda: recv_a[c], x32, o32, put)
        mine = pl.ds(pl.multiple_of(me * LANES, LANES), LANES)
        pltpu.make_async_copy(send_b.at[c, me], out.at[:, c, :, mine], b_recv.at[c]).start()

        def push(k, carry):
            to = lax.rem(me + k, 32)
            pltpu.make_async_remote_copy(
                send_b.at[c, to], out.at[:, c, :, mine], b_send.at[c], b_recv.at[c],
                device_id=(to, z), device_id_type=MESH,
            ).start()
            return carry

        lax.fori_loop(1, 32, push, 0)

    def halves(h, carry):
        @pl.when(h == 1)
        def _():
            for halo in halos:
                halo.wait()

            @pl.when(z == 0)
            def _():
                sx[:, :, 0] = jnp.zeros((2, 2, ORB, ORB), BF)

            @pl.when(z == 7)
            def _():
                sx[:, :, 5] = jnp.zeros((2, 2, ORB, ORB), BF)

        def first(i, carry):
            lesser(jnp.where(h == 0, 1 + i, 3 * i))
            return carry

        lax.fori_loop(0, 2, first, 0)

        @pl.when(h == 0)
        def _():
            build_kernels(screened, kmat)

        def second(i, carry):
            convolve(jnp.where(h == 0, 1 + i, 3 * i))
            return carry

        return lax.fori_loop(0, 2, second, carry)

    lax.fori_loop(0, 2, halves, 0)
    for c in range(4):
        pltpu.make_async_copy(out.at[:, c], out.at[:, c], b_recv.at[c]).wait()
        sent = send_a.at[c, pl.ds(0, 31)]
        pltpu.make_async_copy(sent, sent, a_send.at[c]).wait()
        sent = send_b.at[c, pl.ds(0, 31)]
        pltpu.make_async_copy(sent, sent, b_send.at[c]).wait()


VM = pl.BlockSpec(memory_space=pltpu.VMEM)
SM = pl.BlockSpec(memory_space=pltpu.SMEM)
ANY = pl.BlockSpec(memory_space=pl.ANY)
MESH = pl.DeviceIdType.MESH


def per_device(gd, gl, gu, s, screened, kept, count):
    big = pltpu.VMEM((2, 2, 4, ORB, ORB), BF)
    dma = pltpu.SemaphoreType.DMA
    out = pl.pallas_call(
        whole,
        out_shape=jax.ShapeDtypeStruct((4, 4, KMAX, SUB * SUB), BF),
        in_specs=[SM, SM, VM, ANY, ANY, ANY, ANY],
        out_specs=ANY,
        scratch_shapes=[
            big,
            big,
            big,
            pltpu.VMEM((2, 2, 6, ORB, ORB), BF),
            pltpu.VMEM((16, SUB, LANES), F32),
            pltpu.VMEM((16, SUB, LANES), F32),
            pltpu.VMEM((4, 32, 2, 16, LANES), BF),
            pltpu.VMEM((4, 32, 2, 16, LANES), BF),
            pltpu.VMEM((4, LANES, LANES), BF),
            pltpu.VMEM((32, 2, 16, LANES), F32),
            pltpu.VMEM((LANES, KMAX, LANES), F32),
            pltpu.VMEM((4, 32, 4, KMAX, LANES), BF),
            dma((4, 3)),
            dma(()),
            dma((2,)),
            dma((2,)),
            dma((4,)),
            dma((4,)),
            dma((4,)),
            dma((4,)),
        ],
        compiler_params=pltpu.CompilerParams(
            vmem_limit_bytes=60 * 1024 * 1024, collective_id=0, has_side_effects=True
        ),
        name="whole",
    )(kept, count, screened, gd, gl, gu, s)
    return out.reshape(2, 2, 4, KMAX, SUB * SUB)


def solution(mesh):
    placed = P(None, "energy", "cell", None, None)
    return jax.shard_map(
        per_device,
        mesh=mesh,
        in_specs=(placed, placed, placed, placed, P(None, "cell", None), P("cell", None), P("cell")),
        out_specs=placed,
        check_vma=False,
    )
```

```python
import jax
import jax.numpy as jnp
from jax import lax
from jax.experimental import pallas as pl
from jax.experimental.pallas import tpu as pltpu
from jax.sharding import PartitionSpec as P

ORB = 256
SUB = 64
KMAX = 8
LANES = 128
BF = jnp.bfloat16
F32 = jnp.float32


def mm(a, b):
    return jnp.dot(a, b, preferred_element_type=F32)


def mm_t(a, b):
    return lax.dot_general(a, b, (((1,), (1,)), ((), ())), preferred_element_type=F32)


def one_side(gr, gi, sr, si):
    inner_r = mm(jnp.concatenate([gr, -gi], 1), jnp.concatenate([sr, si], 0)).astype(BF)
    inner_i = mm(jnp.concatenate([gr, gi], 1), jnp.concatenate([si, sr], 0)).astype(BF)
    rows = []
    for b in range(ORB // SUB):
        part = slice(b * SUB, (b + 1) * SUB)
        rows.append(jnp.concatenate([gr[part], gi[part]], 1))
        rows.append(jnp.concatenate([-gi[part], gr[part]], 1))
    return mm_t(jnp.concatenate([inner_r, inner_i], 1), jnp.concatenate(rows, 0))


def side(c, e, k, at, vg, sx):
    return one_side(vg[k, 0, e, c], vg[k, 1, e, c], sx[0, e, at], sx[1, e, at])


def store_blocks(total, part):
    for rb in range(ORB // SUB):
        for cb in range(ORB // SUB):
            part[rb * 4 + cb] = total[rb * SUB : (rb + 1) * SUB, cb * LANES : (cb + 1) * LANES]


def select(c, e, kept, count, part, sel32):
    live = count[c]
    for j in range(KMAX):
        rows = pl.ds(pl.multiple_of((j * 2 + e) * SUB, SUB), SUB)
        sel32[rows, :] = part[kept[c, j]] * jnp.where(j < live, 1.0, 0.0).astype(F32)


def pack(sel32, put):
    low = iota((16, LANES), 1) < SUB
    for d in range(32):
        even = sel32[pl.ds(2 * d, 16, stride=SUB), :]
        odd = sel32[pl.ds(2 * d + 1, 16, stride=SUB), :]
        put(d, 0, jnp.where(low, even, pltpu.roll(odd, SUB, 1)).astype(BF))
        put(d, 1, jnp.where(low, pltpu.roll(even, SUB, 1), odd).astype(BF))


def iota(shape, dim):
    return lax.broadcasted_iota(jnp.int32, shape, dim)


def build_kernels(screened, kmat):
    shape = (LANES, LANES)
    flip = (iota(shape, 0) == 126 - iota(shape, 1)).astype(BF)
    row, col = iota(shape, 0), iota(shape, 1)
    source = ((row // 2) % 2) * 64 + (row // 4) * 2 + row % 2
    row_pick = (source == col).astype(BF)
    wanted = (col // 64) * 64 + (col % 32) * 2 + (col // 32) % 2
    col_pick = (wanted == row).astype(BF)
    srow = iota((256, LANES), 0)
    low = iota((64, LANES), 1) < 64
    rev = mm(jnp.concatenate([screened[0], screened[1]], 0), flip)
    halves = []
    for p in range(2):
        rows = [jnp.broadcast_to(rev[4 * p + c : 4 * p + c + 1], (64, LANES)) for c in range(4)]
        x = pltpu.roll(jnp.concatenate(rows, 0), 65, 1)
        for bit in range(6):
            x = jnp.where((srow >> bit) % 2 == 1, pltpu.roll(x, 1 << bit, 1), x)
        halves.append(x)
    natural = []
    for c in range(4):
        kr, ki = (half[c * 64 : c * 64 + 64] for half in halves)
        top = jnp.where(low, kr, pltpu.roll(-ki, 64, 1))
        bottom = jnp.where(low, ki, pltpu.roll(kr, 64, 1))
        natural.append(jnp.concatenate([top, bottom], 0).astype(BF))
    picked = mm(row_pick, jnp.concatenate(natural, 1)).astype(BF)
    stacked = jnp.concatenate([picked[:, c * LANES : (c + 1) * LANES] for c in range(4)], 0)
    done = mm(stacked, col_pick).astype(BF)
    for c in range(4):
        kmat[c] = done[c * LANES : (c + 1) * LANES]


def conv_cell(kc, get, x32, o32, put):
    x32[...] = get().astype(F32).reshape(1024, LANES)
    for j in range(KMAX):
        parts = []
        for p in range(2):
            for e2 in range(2):
                parts.append(x32[pl.ds(p * 16 + 2 * j + e2, 32, stride=32), :].astype(BF))
        o32[pl.ds(j, LANES, stride=KMAX), :] = mm(kc, jnp.concatenate(parts, 0))
    put(o32[...].astype(BF))


def whole(kept, count, screened, gd, gl, gu, s, out, vg, sx, part, sel32, send_a, recv_a, kmat, x32, o32, send_b,
          in_sem, s_sem, halo_send, halo_recv, a_send, a_recv, b_send, b_recv):
    me = lax.axis_index("energy")
    z = lax.axis_index("cell")
    up = lax.rem(z + 1, 8)
    down = lax.rem(z + 7, 8)

    def inputs(c):
        here = pl.ds(c, 1)
        return [
            pltpu.make_async_copy(g.at[:, :, here], vg.at[k, :, :, here], in_sem.at[c, k])
            for k, g in enumerate((gd, gl, gu))
        ]

    own = pltpu.make_async_copy(s, sx.at[:, :, pl.ds(1, 4)], s_sem)
    own.start()
    for c in (1, 2, 0, 3):
        for copy in inputs(c):
            copy.start()

    barrier = pltpu.get_barrier_semaphore()
    pl.semaphore_signal(barrier, 1, device_id=(me, up), device_id_type=MESH)
    pl.semaphore_signal(barrier, 1, device_id=(me, down), device_id_type=MESH)

    def greet(k, carry):
        pl.semaphore_signal(barrier, 1, device_id=(lax.rem(me + k, 32), z), device_id_type=MESH)
        return carry

    lax.fori_loop(1, 32, greet, 0)
    build_kernels(screened, kmat)
    pl.semaphore_wait(barrier, 33)

    halos = [
        pltpu.make_async_remote_copy(
            s.at[:, :, pl.ds(source, 1)], sx.at[:, :, pl.ds(target, 1)], halo_send.at[k], halo_recv.at[k],
            device_id=(me, where), device_id_type=MESH,
        )
        for k, (source, target, where) in enumerate(((3, 0, up), (0, 5, down)))
    ]
    for halo in halos:
        halo.start()
    own.wait()

    def send_cell(c):
        def put(d, p, value):
            send_a[c, d, p] = value

        pack(sel32, put)
        pltpu.make_async_copy(send_a.at[c, me], recv_a.at[c, me], a_recv.at[c]).start()

        def push(k, carry):
            to = lax.rem(me + k, 32)
            pltpu.make_async_remote_copy(
                send_a.at[c, to], recv_a.at[c, me], a_send.at[c], a_recv.at[c],
                device_id=(to, z), device_id_type=MESH,
            ).start()
            return carry

        lax.fori_loop(1, 32, push, 0)

    def convolve(c):
        pltpu.make_async_copy(recv_a.at[c], recv_a.at[c], a_recv.at[c]).wait()

        def put(value):
            send_b[c] = value.reshape(32, 4, KMAX, LANES)

        conv_cell(kmat[c], lambda: recv_a[c], x32, o32, put)
        mine = pl.ds(pl.multiple_of(me * LANES, LANES), LANES)
        pltpu.make_async_copy(send_b.at[c, me], out.at[:, c, :, mine], b_recv.at[c]).start()

        def push(k, carry):
            to = lax.rem(me + k, 32)
            pltpu.make_async_remote_copy(
                send_b.at[c, to], out.at[:, c, :, mine], b_send.at[c], b_recv.at[c],
                device_id=(to, z), device_id_type=MESH,
            ).start()
            return carry

        lax.fori_loop(1, 32, push, 0)

    def inner_cell(i, carry):
        c = 1 + i
        for copy in inputs(c):
            copy.wait()

        def energy(e, carry):
            total = side(c, e, 0, c + 1, vg, sx) + side(c, e, 1, c, vg, sx) + side(c, e, 2, c + 2, vg, sx)
            store_blocks(total, part.at[0, e])
            select(c, e, kept, count, part.at[0, e], sel32)
            return carry

        lax.fori_loop(0, 2, energy, 0)
        send_cell(c)
        return carry

    def edge_start(i, carry):
        c = 3 * i
        for copy in inputs(c):
            copy.wait()

        def energy(e, carry):
            store_blocks(side(c, e, 0, c + 1, vg, sx) + side(c, e, 2 - i, 2 + i, vg, sx), part.at[i, e])
            return carry

        lax.fori_loop(0, 2, energy, 0)
        convolve(1 + i)
        return carry

    def edge_end(i, carry):
        c = 3 * i
        inside = jnp.where(z == 7 * i, 0.0, 1.0).astype(BF)

        def energy(e, carry):
            at = 5 * i
            total = one_side(vg[1 + i, 0, e, c], vg[1 + i, 1, e, c], sx[0, e, at] * inside, sx[1, e, at] * inside)
            for rb in range(ORB // SUB):
                for cb in range(ORB // SUB):
                    block = total[rb * SUB : (rb + 1) * SUB, cb * LANES : (cb + 1) * LANES]
                    part[i, e, rb * 4 + cb] += block
            select(c, e, kept, count, part.at[i, e], sel32)
            return carry

        lax.fori_loop(0, 2, energy, 0)
        send_cell(c)
        return carry

    def edge_convolve(i, carry):
        convolve(3 * i)
        return carry

    lax.fori_loop(0, 2, inner_cell, 0)
    lax.fori_loop(0, 2, edge_start, 0)
    for halo in halos:
        halo.wait()
    lax.fori_loop(0, 2, edge_end, 0)
    lax.fori_loop(0, 2, edge_convolve, 0)
    for c in range(4):
        pltpu.make_async_copy(out.at[:, c], out.at[:, c], b_recv.at[c]).wait()
        sent = send_a.at[c, pl.ds(0, 31)]
        pltpu.make_async_copy(sent, sent, a_send.at[c]).wait()
        sent = send_b.at[c, pl.ds(0, 31)]
        pltpu.make_async_copy(sent, sent, b_send.at[c]).wait()


VM = pl.BlockSpec(memory_space=pltpu.VMEM)
SM = pl.BlockSpec(memory_space=pltpu.SMEM)
ANY = pl.BlockSpec(memory_space=pl.ANY)
MESH = pl.DeviceIdType.MESH


def per_device(gd, gl, gu, s, screened, kept, count):
    dma = pltpu.SemaphoreType.DMA
    out = pl.pallas_call(
        whole,
        out_shape=pltpu.VMEM((4, 4, KMAX, SUB * SUB), BF),
        in_specs=[SM, SM, VM, ANY, ANY, ANY, ANY],
        out_specs=VM,
        scratch_shapes=[
            pltpu.VMEM((3, 2, 2, 4, ORB, ORB), BF),
            pltpu.VMEM((2, 2, 6, ORB, ORB), BF),
            pltpu.VMEM((2, 2, 16, SUB, LANES), F32),
            pltpu.VMEM((16 * SUB, LANES), F32),
            pltpu.VMEM((4, 32, 2, 16, LANES), BF),
            pltpu.VMEM((4, 32, 2, 16, LANES), BF),
            pltpu.VMEM((4, LANES, LANES), BF),
            pltpu.VMEM((32 * 32, LANES), F32),
            pltpu.VMEM((LANES * KMAX, LANES), F32),
            pltpu.VMEM((4, 32, 4, KMAX, LANES), BF),
            dma((4, 3)),
            dma(()),
            dma((2,)),
            dma((2,)),
            dma((4,)),
            dma((4,)),
            dma((4,)),
            dma((4,)),
        ],
        compiler_params=pltpu.CompilerParams(
            vmem_limit_bytes=60 * 1024 * 1024, collective_id=0, has_side_effects=True
        ),
        name="whole",
    )(kept, count, screened, gd, gl, gu, s)
    return out.reshape(2, 2, 4, KMAX, SUB * SUB)


def solution(mesh):
    placed = P(None, "energy", "cell", None, None)
    return jax.shard_map(
        per_device,
        mesh=mesh,
        in_specs=(placed, placed, placed, placed, P(None, "cell", None), P("cell", None), P("cell")),
        out_specs=placed,
        check_vma=False,
    )
```

```python
import jax
import jax.numpy as jnp
from jax import lax
from jax.experimental import pallas as pl
from jax.experimental.pallas import tpu as pltpu
from jax.sharding import PartitionSpec as P

ORB = 256
SUB = 64
KMAX = 8
LANES = 128
BF = jnp.bfloat16
F32 = jnp.float32


def mm(a, b):
    return jnp.dot(a, b, preferred_element_type=F32)


def mm_t(a, b):
    return lax.dot_general(a, b, (((1,), (1,)), ((), ())), preferred_element_type=F32)


def one_side(gr, gi, sr, si):
    inner_r = mm(jnp.concatenate([gr, -gi], 1), jnp.concatenate([sr, si], 0)).astype(BF)
    inner_i = mm(jnp.concatenate([gr, gi], 1), jnp.concatenate([si, sr], 0)).astype(BF)
    rows = []
    for b in range(ORB // SUB):
        part = slice(b * SUB, (b + 1) * SUB)
        rows.append(jnp.concatenate([gr[part], gi[part]], 1))
        rows.append(jnp.concatenate([-gi[part], gr[part]], 1))
    return mm_t(jnp.concatenate([inner_r, inner_i], 1), jnp.concatenate(rows, 0))


def side(c, e, k, at, vg, sx):
    return one_side(vg[k, 0, e, c], vg[k, 1, e, c], sx[0, e, at], sx[1, e, at])


def store_blocks(total, part):
    for rb in range(ORB // SUB):
        for cb in range(ORB // SUB):
            part[rb * 4 + cb] = total[rb * SUB : (rb + 1) * SUB, cb * LANES : (cb + 1) * LANES]


def select(c, e, kept, count, part, sel32):
    live = count[c]
    for j in range(KMAX):
        rows = pl.ds(pl.multiple_of((e * KMAX + j) * SUB, SUB), SUB)
        sel32[rows, :] = part[kept[c, j]] * jnp.where(j < live, 1.0, 0.0).astype(F32)


def pack(c, e, sel32, send):
    low = iota((KMAX, LANES), 1) < SUB
    for d in range(32):
        even = sel32[pl.ds(e * (KMAX * SUB) + 2 * d, KMAX, stride=SUB), :]
        odd = sel32[pl.ds(e * (KMAX * SUB) + 2 * d + 1, KMAX, stride=SUB), :]
        send[c, d, e, 0] = jnp.where(low, even, pltpu.roll(odd, SUB, 1)).astype(BF)
        send[c, d, e, 1] = jnp.where(low, pltpu.roll(even, SUB, 1), odd).astype(BF)


def iota(shape, dim):
    return lax.broadcasted_iota(jnp.int32, shape, dim)


def build_kernels(screened, kmat):
    shape = (LANES, LANES)
    flip = (iota(shape, 0) == 126 - iota(shape, 1)).astype(BF)
    row, col = iota(shape, 0), iota(shape, 1)
    source = ((row // 2) % 2) * 64 + (row // 4) * 2 + row % 2
    row_pick = (source == col).astype(BF)
    wanted = (col // 64) * 64 + (col % 32) * 2 + (col // 32) % 2
    col_pick = (wanted == row).astype(BF)
    srow = iota((256, LANES), 0)
    low = iota((64, LANES), 1) < 64
    rev = mm(jnp.concatenate([screened[0], screened[1]], 0), flip)
    halves = []
    for p in range(2):
        rows = [jnp.broadcast_to(rev[4 * p + c : 4 * p + c + 1], (64, LANES)) for c in range(4)]
        x = pltpu.roll(jnp.concatenate(rows, 0), 65, 1)
        for bit in range(6):
            x = jnp.where((srow >> bit) % 2 == 1, pltpu.roll(x, 1 << bit, 1), x)
        halves.append(x)
    natural = []
    for c in range(4):
        kr, ki = (half[c * 64 : c * 64 + 64] for half in halves)
        top = jnp.where(low, kr, pltpu.roll(-ki, 64, 1))
        bottom = jnp.where(low, ki, pltpu.roll(kr, 64, 1))
        natural.append(jnp.concatenate([top, bottom], 0).astype(BF))
    picked = mm(row_pick, jnp.concatenate(natural, 1)).astype(BF)
    stacked = jnp.concatenate([picked[:, c * LANES : (c + 1) * LANES] for c in range(4)], 0)
    done = mm(stacked, col_pick).astype(BF)
    for c in range(4):
        kmat[c] = done[c * LANES : (c + 1) * LANES]


def conv_cell(kc, get, x32, o32, put):
    x32[...] = get().astype(F32).reshape(1024, LANES)
    for j in range(KMAX):
        parts = []
        for p in range(2):
            for e2 in range(2):
                parts.append(x32[pl.ds(e2 * 16 + p * KMAX + j, 32, stride=32), :].astype(BF))
        o32[pl.ds(j, LANES, stride=KMAX), :] = mm(kc, jnp.concatenate(parts, 0))
    put(o32[...].astype(BF))


def whole(kept, count, screened, gd, gl, gu, s, out, vg, sx, part, sel32, send_a, recv_a, kmat, x32, o32, send_b,
          in_sem, s_sem, halo_send, halo_recv, a_send, a_recv, b_send, b_recv):
    me = lax.axis_index("energy")
    z = lax.axis_index("cell")
    up = lax.rem(z + 1, 8)
    down = lax.rem(z + 7, 8)

    def inputs(c):
        here = pl.ds(c, 1)
        return [
            pltpu.make_async_copy(g.at[:, :, here], vg.at[k, :, :, here], in_sem.at[c, k])
            for k, g in enumerate((gd, gl, gu))
        ]

    own = pltpu.make_async_copy(s, sx.at[:, :, pl.ds(1, 4)], s_sem)
    own.start()
    for c in (1, 2, 0, 3):
        for copy in inputs(c):
            copy.start()

    barrier = pltpu.get_barrier_semaphore()
    pl.semaphore_signal(barrier, 1, device_id=(me, up), device_id_type=MESH)
    pl.semaphore_signal(barrier, 1, device_id=(me, down), device_id_type=MESH)

    def greet(k, carry):
        pl.semaphore_signal(barrier, 1, device_id=(lax.rem(me + k, 32), z), device_id_type=MESH)
        return carry

    lax.fori_loop(1, 32, greet, 0)
    pl.semaphore_wait(barrier, 33)

    halos = [
        pltpu.make_async_remote_copy(
            s.at[:, pl.ds(e, 1), pl.ds(source, 1)], sx.at[:, pl.ds(e, 1), pl.ds(target, 1)],
            halo_send.at[e, k], halo_recv.at[e, k], device_id=(me, where), device_id_type=MESH,
        )
        for e in range(2)
        for k, (source, target, where) in enumerate(((3, 0, up), (0, 5, down)))
    ]
    for halo in halos:
        halo.start()
    own.wait()

    def push(c, outgoing, arriving):
        pltpu.make_async_copy(outgoing(me), arriving, a_recv.at[c]).start()

        def one(k, carry):
            to = lax.rem(me + k, 32)
            pltpu.make_async_remote_copy(
                outgoing(to), arriving, a_send.at[c], a_recv.at[c], device_id=(to, z), device_id_type=MESH
            ).start()
            return carry

        lax.fori_loop(1, 32, one, 0)

    def send_cell(c):
        push(c, lambda d: send_a.at[c, d], recv_a.at[c, me])

    def convolve(c):
        pltpu.make_async_copy(recv_a.at[c], recv_a.at[c], a_recv.at[c]).wait()

        def put(value):
            send_b[c] = value.reshape(32, 4, KMAX, LANES)

        conv_cell(kmat[c], lambda: recv_a[c], x32, o32, put)
        mine = pl.ds(pl.multiple_of(me * LANES, LANES), LANES)
        pltpu.make_async_copy(send_b.at[c, me], out.at[:, c, :, mine], b_recv.at[c]).start()

        def push(k, carry):
            to = lax.rem(me + k, 32)
            pltpu.make_async_remote_copy(
                send_b.at[c, to], out.at[:, c, :, mine], b_send.at[c], b_recv.at[c],
                device_id=(to, z), device_id_type=MESH,
            ).start()
            return carry

        lax.fori_loop(1, 32, push, 0)

    def both(work):
        def energy(e, carry):
            work(e)
            return carry

        lax.fori_loop(0, 2, energy, 0)

    def inner_cell(i, carry):
        c = 1 + i
        for copy in inputs(c):
            copy.wait()

        def work(e):
            total = side(c, e, 0, c + 1, vg, sx) + side(c, e, 1, c, vg, sx) + side(c, e, 2, c + 2, vg, sx)
            store_blocks(total, part.at[0, e])
            select(c, e, kept, count, part.at[0, e], sel32)
            pack(c, e, sel32, send_a)

        both(work)
        send_cell(c)
        return carry

    def edge_start(i, carry):
        c = 3 * i
        for copy in inputs(c):
            copy.wait()

        def work(e):
            store_blocks(side(c, e, 0, c + 1, vg, sx) + side(c, e, 2 - i, 2 + i, vg, sx), part.at[i, e])

        both(work)

        @pl.when(z == 7 * i)
        def _():
            def finish(e):
                select(c, e, kept, count, part.at[i, e], sel32)
                pack(c, e, sel32, send_a)

            both(finish)
            send_cell(c)

        return carry

    def edge_end(e):
        def one(i, carry):
            c = 3 * i

            @pl.when(z != 7 * i)
            def _():
                total = side(c, e, 1 + i, 5 * i, vg, sx)
                for rb in range(ORB // SUB):
                    for cb in range(ORB // SUB):
                        block = total[rb * SUB : (rb + 1) * SUB, cb * LANES : (cb + 1) * LANES]
                        part[i, e, rb * 4 + cb] += block
                select(c, e, kept, count, part.at[i, e], sel32)
                pack(c, e, sel32, send_a)
                push(c, lambda d: send_a.at[c, d, e], recv_a.at[c, me, e])

            return carry

        lax.fori_loop(0, 2, one, 0)

    lax.fori_loop(0, 2, inner_cell, 0)
    build_kernels(screened, kmat)
    lax.fori_loop(0, 2, edge_start, 0)

    def tail(e, carry):
        for k in range(2):
            pltpu.make_async_copy(
                sx.at[:, pl.ds(e, 1), pl.ds(5 * k, 1)], sx.at[:, pl.ds(e, 1), pl.ds(5 * k, 1)], halo_recv.at[e, k]
            ).wait()
        edge_end(e)
        convolve(1 + e)
        return carry

    lax.fori_loop(0, 2, tail, 0)

    def edge_convolve(i, carry):
        convolve(3 * i)
        return carry

    lax.fori_loop(0, 2, edge_convolve, 0)
    for halo in halos:
        halo.wait_send()
    for c in range(4):
        pltpu.make_async_copy(out.at[:, c], out.at[:, c], b_recv.at[c]).wait()
        sent = send_a.at[c, pl.ds(0, 31)]
        pltpu.make_async_copy(sent, sent, a_send.at[c]).wait()
        sent = send_b.at[c, pl.ds(0, 31)]
        pltpu.make_async_copy(sent, sent, b_send.at[c]).wait()


VM = pl.BlockSpec(memory_space=pltpu.VMEM)
SM = pl.BlockSpec(memory_space=pltpu.SMEM)
ANY = pl.BlockSpec(memory_space=pl.ANY)
MESH = pl.DeviceIdType.MESH


def per_device(gd, gl, gu, s, screened, kept, count):
    dma = pltpu.SemaphoreType.DMA
    out = pl.pallas_call(
        whole,
        out_shape=pltpu.VMEM((4, 4, KMAX, SUB * SUB), BF),
        in_specs=[SM, SM, VM, ANY, ANY, ANY, ANY],
        out_specs=VM,
        scratch_shapes=[
            pltpu.VMEM((3, 2, 2, 4, ORB, ORB), BF),
            pltpu.VMEM((2, 2, 6, ORB, ORB), BF),
            pltpu.VMEM((2, 2, 16, SUB, LANES), F32),
            pltpu.VMEM((16 * SUB, LANES), F32),
            pltpu.VMEM((4, 32, 2, 2, KMAX, LANES), BF),
            pltpu.VMEM((4, 32, 2, 2, KMAX, LANES), BF),
            pltpu.VMEM((4, LANES, LANES), BF),
            pltpu.VMEM((32 * 32, LANES), F32),
            pltpu.VMEM((LANES * KMAX, LANES), F32),
            pltpu.VMEM((4, 32, 4, KMAX, LANES), BF),
            dma((4, 3)),
            dma(()),
            dma((2, 2)),
            dma((2, 2)),
            dma((4,)),
            dma((4,)),
            dma((4,)),
            dma((4,)),
        ],
        compiler_params=pltpu.CompilerParams(
            vmem_limit_bytes=60 * 1024 * 1024, collective_id=0, has_side_effects=True
        ),
        name="whole",
    )(kept, count, screened, gd, gl, gu, s)
    return out.reshape(2, 2, 4, KMAX, SUB * SUB)


def solution(mesh):
    placed = P(None, "energy", "cell", None, None)
    return jax.shard_map(
        per_device,
        mesh=mesh,
        in_specs=(placed, placed, placed, placed, P(None, "cell", None), P("cell", None), P("cell")),
        out_specs=placed,
        check_vma=False,
    )
```

```python
import jax
import jax.numpy as jnp
from jax import lax
from jax.experimental import pallas as pl
from jax.experimental.pallas import tpu as pltpu
from jax.sharding import PartitionSpec as P

ORB = 256
SUB = 64
KMAX = 8
LANES = 128
BF = jnp.bfloat16
F32 = jnp.float32


def mm(a, b):
    return jnp.dot(a, b, preferred_element_type=F32)


def mm_t(a, b):
    return lax.dot_general(a, b, (((1,), (1,)), ((), ())), preferred_element_type=F32)


def one_side(gr, gi, sr, si):
    inner_r = mm(jnp.concatenate([gr, -gi], 1), jnp.concatenate([sr, si], 0)).astype(BF)
    inner_i = mm(jnp.concatenate([gr, gi], 1), jnp.concatenate([si, sr], 0)).astype(BF)
    rows = []
    for b in range(ORB // SUB):
        part = slice(b * SUB, (b + 1) * SUB)
        rows.append(jnp.concatenate([gr[part], gi[part]], 1))
        rows.append(jnp.concatenate([-gi[part], gr[part]], 1))
    return mm_t(jnp.concatenate([inner_r, inner_i], 1), jnp.concatenate(rows, 0))


def side(c, e, k, at, vg, sx):
    return one_side(vg[k, 0, e, c], vg[k, 1, e, c], sx[0, e, at], sx[1, e, at])


def store_blocks(total, part):
    for rb in range(ORB // SUB):
        for cb in range(ORB // SUB):
            part[rb * 4 + cb] = total[rb * SUB : (rb + 1) * SUB, cb * LANES : (cb + 1) * LANES]


def select(c, e, kept, count, part, sel32):
    live = count[c]
    for j in range(KMAX):
        rows = pl.ds(pl.multiple_of((e * KMAX + j) * SUB, SUB), SUB)
        sel32[rows, :] = part[kept[c, j]] * jnp.where(j < live, 1.0, 0.0).astype(F32)


def pack(c, e, sel32, send):
    low = iota((KMAX, LANES), 1) < SUB
    for d in range(32):
        even = sel32[pl.ds(e * (KMAX * SUB) + 2 * d, KMAX, stride=SUB), :]
        odd = sel32[pl.ds(e * (KMAX * SUB) + 2 * d + 1, KMAX, stride=SUB), :]
        send[c, d, e, 0] = jnp.where(low, even, pltpu.roll(odd, SUB, 1)).astype(BF)
        send[c, d, e, 1] = jnp.where(low, pltpu.roll(even, SUB, 1), odd).astype(BF)


def iota(shape, dim):
    return lax.broadcasted_iota(jnp.int32, shape, dim)


def build_kernels(screened, kmat):
    shape = (LANES, LANES)
    flip = (iota(shape, 0) == 126 - iota(shape, 1)).astype(BF)
    row, col = iota(shape, 0), iota(shape, 1)
    source = ((row // 2) % 2) * 64 + (row // 4) * 2 + row % 2
    row_pick = (source == col).astype(BF)
    wanted = (col // 64) * 64 + (col % 32) * 2 + (col // 32) % 2
    col_pick = (wanted == row).astype(BF)
    srow = iota((256, LANES), 0)
    low = iota((64, LANES), 1) < 64
    rev = mm(jnp.concatenate([screened[0], screened[1]], 0), flip)
    halves = []
    for p in range(2):
        rows = [jnp.broadcast_to(rev[4 * p + c : 4 * p + c + 1], (64, LANES)) for c in range(4)]
        x = pltpu.roll(jnp.concatenate(rows, 0), 65, 1)
        for bit in range(6):
            x = jnp.where((srow >> bit) % 2 == 1, pltpu.roll(x, 1 << bit, 1), x)
        halves.append(x)
    natural = []
    for c in range(4):
        kr, ki = (half[c * 64 : c * 64 + 64] for half in halves)
        top = jnp.where(low, kr, pltpu.roll(-ki, 64, 1))
        bottom = jnp.where(low, ki, pltpu.roll(kr, 64, 1))
        natural.append(jnp.concatenate([top, bottom], 0).astype(BF))
    picked = mm(row_pick, jnp.concatenate(natural, 1)).astype(BF)
    stacked = jnp.concatenate([picked[:, c * LANES : (c + 1) * LANES] for c in range(4)], 0)
    done = mm(stacked, col_pick).astype(BF)
    for c in range(4):
        kmat[c] = done[c * LANES : (c + 1) * LANES]


def conv_cell(kc, get, x32, o32, put):
    x32[...] = get().astype(F32).reshape(1024, LANES)
    for j in range(KMAX):
        parts = []
        for p in range(2):
            for e2 in range(2):
                parts.append(x32[pl.ds(e2 * 16 + p * KMAX + j, 32, stride=32), :].astype(BF))
        o32[pl.ds(j, LANES, stride=KMAX), :] = mm(kc, jnp.concatenate(parts, 0))
    put(o32[...].astype(BF))


def far_first(me):
    x, y, core = me // 8, me // 2 % 4, me % 2
    hops = (0, 1, 2, 1)
    steps = [(a, b, c) for a in range(4) for b in range(4) for c in range(2)][1:]
    steps.sort(key=lambda o: (-hops[o[0]] - hops[o[1]], o))
    return [(x + a) % 4 * 8 + (y + b) % 4 * 2 + (core + c) % 2 for a, b, c in steps]


def whole(kept, count, screened, gd, gl, gu, s, out, vg, sx, part, sel32, send_a, recv_a, kmat, x32, o32, send_b,
          in_sem, s_sem, halo_send, halo_recv, a_send, a_recv, b_send, b_recv):
    me = lax.axis_index("energy")
    z = lax.axis_index("cell")
    targets = far_first(me)
    up = lax.rem(z + 1, 8)
    down = lax.rem(z + 7, 8)

    def inputs(c):
        here = pl.ds(c, 1)
        return [
            pltpu.make_async_copy(g.at[:, :, here], vg.at[k, :, :, here], in_sem.at[c, k])
            for k, g in enumerate((gd, gl, gu))
        ]

    own = pltpu.make_async_copy(s, sx.at[:, :, pl.ds(1, 4)], s_sem)
    own.start()
    for c in (1, 2, 0, 3):
        for copy in inputs(c):
            copy.start()

    barrier = pltpu.get_barrier_semaphore()
    pl.semaphore_signal(barrier, 1, device_id=(me, up), device_id_type=MESH)
    pl.semaphore_signal(barrier, 1, device_id=(me, down), device_id_type=MESH)

    def greet(k, carry):
        pl.semaphore_signal(barrier, 1, device_id=(lax.rem(me + k, 32), z), device_id_type=MESH)
        return carry

    lax.fori_loop(1, 32, greet, 0)
    pl.semaphore_wait(barrier, 33)

    halos = [
        pltpu.make_async_remote_copy(
            s.at[:, pl.ds(e, 1), pl.ds(source, 1)], sx.at[:, pl.ds(e, 1), pl.ds(target, 1)],
            halo_send.at[e, k], halo_recv.at[e, k], device_id=(me, where), device_id_type=MESH,
        )
        for e in range(2)
        for k, (source, target, where) in enumerate(((3, 0, up), (0, 5, down)))
    ]
    for halo in halos:
        halo.start()
    build_kernels(screened, kmat)
    own.wait()

    def send_energy(c, e, source):
        select(c, e, kept, count, source, sel32)
        pack(c, e, sel32, send_a)
        pltpu.make_async_copy(send_a.at[c, me, e], recv_a.at[c, me, e], a_recv.at[c]).start()

        for to in targets:
            pltpu.make_async_remote_copy(
                send_a.at[c, to, e], recv_a.at[c, me, e], a_send.at[c], a_recv.at[c],
                device_id=(to, z), device_id_type=MESH,
            ).start()

    def convolve(c):
        pltpu.make_async_copy(recv_a.at[c], recv_a.at[c], a_recv.at[c]).wait()

        def put(value):
            send_b[c] = value.reshape(32, 4, KMAX, LANES)

        conv_cell(kmat[c], lambda: recv_a[c], x32, o32, put)
        mine = pl.ds(pl.multiple_of(me * LANES, LANES), LANES)
        pltpu.make_async_copy(send_b.at[c, me], out.at[:, c, :, mine], b_recv.at[c]).start()

        for to in targets:
            pltpu.make_async_remote_copy(
                send_b.at[c, to], out.at[:, c, :, mine], b_send.at[c], b_recv.at[c],
                device_id=(to, z), device_id_type=MESH,
            ).start()

    def both(work):
        def energy(e, carry):
            work(e)
            return carry

        lax.fori_loop(0, 2, energy, 0)

    def inner_cell(i, carry):
        c = 1 + i
        for copy in inputs(c):
            copy.wait()

        def work(e):
            total = side(c, e, 0, c + 1, vg, sx) + side(c, e, 1, c, vg, sx) + side(c, e, 2, c + 2, vg, sx)
            store_blocks(total, part.at[0, e])
            send_energy(c, e, part.at[0, e])

        both(work)
        return carry

    def edge_start(i, carry):
        c = 3 * i
        for copy in inputs(c):
            copy.wait()

        def work(e):
            store_blocks(side(c, e, 0, c + 1, vg, sx) + side(c, e, 2 - i, 2 + i, vg, sx), part.at[i, e])

        both(work)

        @pl.when(z == 7 * i)
        def _():
            both(lambda e: send_energy(c, e, part.at[i, e]))

        @pl.when(i == 0)
        def _():
            convolve(1)

        return carry

    def edge_end(e):
        def one(i, carry):
            c = 3 * i

            @pl.when(z != 7 * i)
            def _():
                total = side(c, e, 1 + i, 5 * i, vg, sx)
                for rb in range(ORB // SUB):
                    for cb in range(ORB // SUB):
                        block = total[rb * SUB : (rb + 1) * SUB, cb * LANES : (cb + 1) * LANES]
                        part[i, e, rb * 4 + cb] += block
                send_energy(c, e, part.at[i, e])

            return carry

        lax.fori_loop(0, 2, one, 0)

    lax.fori_loop(0, 2, inner_cell, 0)
    lax.fori_loop(0, 2, edge_start, 0)

    def tail(e, carry):
        for k in range(2):
            pltpu.make_async_copy(
                sx.at[:, pl.ds(e, 1), pl.ds(5 * k, 1)], sx.at[:, pl.ds(e, 1), pl.ds(5 * k, 1)], halo_recv.at[e, k]
            ).wait()
        edge_end(e)
        return carry

    lax.fori_loop(0, 2, tail, 0)

    def last_cells(i, carry):
        convolve(jnp.where(i == 0, 2, 3 * i - 3))
        return carry

    lax.fori_loop(0, 3, last_cells, 0)
    for halo in halos:
        halo.wait_send()
    for c in range(4):
        pltpu.make_async_copy(out.at[:, c], out.at[:, c], b_recv.at[c]).wait()
        sent = send_a.at[c, pl.ds(0, 31)]
        pltpu.make_async_copy(sent, sent, a_send.at[c]).wait()
        sent = send_b.at[c, pl.ds(0, 31)]
        pltpu.make_async_copy(sent, sent, b_send.at[c]).wait()


VM = pl.BlockSpec(memory_space=pltpu.VMEM)
SM = pl.BlockSpec(memory_space=pltpu.SMEM)
ANY = pl.BlockSpec(memory_space=pl.ANY)
MESH = pl.DeviceIdType.MESH


def per_device(gd, gl, gu, s, screened, kept, count):
    dma = pltpu.SemaphoreType.DMA
    out = pl.pallas_call(
        whole,
        out_shape=pltpu.VMEM((4, 4, KMAX, SUB * SUB), BF),
        in_specs=[SM, SM, VM, ANY, ANY, ANY, ANY],
        out_specs=VM,
        scratch_shapes=[
            pltpu.VMEM((3, 2, 2, 4, ORB, ORB), BF),
            pltpu.VMEM((2, 2, 6, ORB, ORB), BF),
            pltpu.VMEM((2, 2, 16, SUB, LANES), F32),
            pltpu.VMEM((16 * SUB, LANES), F32),
            pltpu.VMEM((4, 32, 2, 2, KMAX, LANES), BF),
            pltpu.VMEM((4, 32, 2, 2, KMAX, LANES), BF),
            pltpu.VMEM((4, LANES, LANES), BF),
            pltpu.VMEM((32 * 32, LANES), F32),
            pltpu.VMEM((LANES * KMAX, LANES), F32),
            pltpu.VMEM((4, 32, 4, KMAX, LANES), BF),
            dma((4, 3)),
            dma(()),
            dma((2, 2)),
            dma((2, 2)),
            dma((4,)),
            dma((4,)),
            dma((4,)),
            dma((4,)),
        ],
        compiler_params=pltpu.CompilerParams(
            vmem_limit_bytes=60 * 1024 * 1024, collective_id=0, has_side_effects=True
        ),
        name="whole",
    )(kept, count, screened, gd, gl, gu, s)
    return out.reshape(2, 2, 4, KMAX, SUB * SUB)


def solution(mesh):
    placed = P(None, "energy", "cell", None, None)
    return jax.shard_map(
        per_device,
        mesh=mesh,
        in_specs=(placed, placed, placed, placed, P(None, "cell", None), P("cell", None), P("cell")),
        out_specs=placed,
        check_vma=False,
    )
```

```python
import jax
import jax.numpy as jnp
from jax import lax
from jax.experimental import pallas as pl
from jax.experimental.pallas import tpu as pltpu
from jax.sharding import PartitionSpec as P

ORB = 256
SUB = 64
KMAX = 8
LANES = 128
BF = jnp.bfloat16
F32 = jnp.float32


def mm(a, b):
    return jnp.dot(a, b, preferred_element_type=F32)


def mm_t(a, b):
    return lax.dot_general(a, b, (((1,), (1,)), ((), ())), preferred_element_type=F32)


def one_side(gr, gi, sr, si):
    inner_r = mm(jnp.concatenate([gr, -gi], 1), jnp.concatenate([sr, si], 0)).astype(BF)
    inner_i = mm(jnp.concatenate([gr, gi], 1), jnp.concatenate([si, sr], 0)).astype(BF)
    rows = []
    for b in range(ORB // SUB):
        part = slice(b * SUB, (b + 1) * SUB)
        rows.append(jnp.concatenate([gr[part], gi[part]], 1))
        rows.append(jnp.concatenate([-gi[part], gr[part]], 1))
    return mm_t(jnp.concatenate([inner_r, inner_i], 1), jnp.concatenate(rows, 0))


def side(c, e, k, at, vg, sx):
    return one_side(vg[k, 0, e, c], vg[k, 1, e, c], sx[0, e, at], sx[1, e, at])


def store_blocks(total, part):
    for rb in range(ORB // SUB):
        for cb in range(ORB // SUB):
            part[rb * 4 + cb] = total[rb * SUB : (rb + 1) * SUB, cb * LANES : (cb + 1) * LANES]


def select(c, e, kept, count, part, sel32):
    live = count[c]
    for j in range(KMAX):
        rows = pl.ds(pl.multiple_of((e * KMAX + j) * SUB, SUB), SUB)
        sel32[rows, :] = part[kept[c, j]] * jnp.where(j < live, 1.0, 0.0).astype(F32)


def pack(c, e, sel32, send):
    low = iota((KMAX, LANES), 1) < SUB
    for d in range(32):
        even = sel32[pl.ds(e * (KMAX * SUB) + 2 * d, KMAX, stride=SUB), :]
        odd = sel32[pl.ds(e * (KMAX * SUB) + 2 * d + 1, KMAX, stride=SUB), :]
        send[c, d, e, 0] = jnp.where(low, even, pltpu.roll(odd, SUB, 1)).astype(BF)
        send[c, d, e, 1] = jnp.where(low, pltpu.roll(even, SUB, 1), odd).astype(BF)


def iota(shape, dim):
    return lax.broadcasted_iota(jnp.int32, shape, dim)


def build_kernels(screened, kmat):
    shape = (LANES, LANES)
    flip = (iota(shape, 0) == 126 - iota(shape, 1)).astype(BF)
    row, col = iota(shape, 0), iota(shape, 1)
    source = ((row // 2) % 2) * 64 + (row // 4) * 2 + row % 2
    row_pick = (source == col).astype(BF)
    wanted = (col // 64) * 64 + (col % 32) * 2 + (col // 32) % 2
    col_pick = (wanted == row).astype(BF)
    srow = iota((256, LANES), 0)
    low = iota((64, LANES), 1) < 64
    rev = mm(jnp.concatenate([screened[0], screened[1]], 0), flip)
    halves = []
    for p in range(2):
        rows = [jnp.broadcast_to(rev[4 * p + c : 4 * p + c + 1], (64, LANES)) for c in range(4)]
        x = pltpu.roll(jnp.concatenate(rows, 0), 65, 1)
        for bit in range(6):
            x = jnp.where((srow >> bit) % 2 == 1, pltpu.roll(x, 1 << bit, 1), x)
        halves.append(x)
    natural = []
    for c in range(4):
        kr, ki = (half[c * 64 : c * 64 + 64] for half in halves)
        top = jnp.where(low, kr, pltpu.roll(-ki, 64, 1))
        bottom = jnp.where(low, ki, pltpu.roll(kr, 64, 1))
        natural.append(jnp.concatenate([top, bottom], 0).astype(BF))
    picked = mm(row_pick, jnp.concatenate(natural, 1)).astype(BF)
    stacked = jnp.concatenate([picked[:, c * LANES : (c + 1) * LANES] for c in range(4)], 0)
    done = mm(stacked, col_pick).astype(BF)
    for c in range(4):
        kmat[c] = done[c * LANES : (c + 1) * LANES]


def conv_cell(kc, get, x32, o32, put):
    x32[...] = get().astype(F32).reshape(1024, LANES)
    for j in range(KMAX):
        parts = []
        for p in range(2):
            for e2 in range(2):
                parts.append(x32[pl.ds(e2 * 16 + p * KMAX + j, 32, stride=32), :].astype(BF))
        o32[pl.ds(j, LANES, stride=KMAX), :] = mm(kc, jnp.concatenate(parts, 0))
    put(o32[...].astype(BF))


def far_first(me):
    x, y, core = me // 8, me // 2 % 4, me % 2
    hops = (0, 1, 2, 1)
    steps = [(a, b, c) for a in range(4) for b in range(4) for c in range(2)][1:]
    steps.sort(key=lambda o: (-hops[o[0]] - hops[o[1]], o))
    return [(x + a) % 4 * 8 + (y + b) % 4 * 2 + (core + c) % 2 for a, b, c in steps]


def whole(kept, count, screened, gd, gl, gu, s, out, vg, sx, part, sel32, send_a, recv_a, kmat, x32, o32, send_b,
          in_sem, s_sem, halo_send, halo_recv, a_send, a_recv, b_send, b_recv):
    me = lax.axis_index("energy")
    z = lax.axis_index("cell")
    targets = far_first(me)
    up = lax.rem(z + 1, 8)
    down = lax.rem(z + 7, 8)

    def inputs(c):
        here = pl.ds(c, 1)
        return [
            pltpu.make_async_copy(g.at[:, :, here], vg.at[k, :, :, here], in_sem.at[c, k])
            for k, g in enumerate((gd, gl, gu))
        ]

    own = pltpu.make_async_copy(s, sx.at[:, :, pl.ds(1, 4)], s_sem)
    own.start()
    for c in (1, 2, 0, 3):
        for copy in inputs(c):
            copy.start()

    barrier = pltpu.get_barrier_semaphore()
    pl.semaphore_signal(barrier, 1, device_id=(me, up), device_id_type=MESH)
    pl.semaphore_signal(barrier, 1, device_id=(me, down), device_id_type=MESH)

    def greet(k, carry):
        pl.semaphore_signal(barrier, 1, device_id=(lax.rem(me + k, 32), z), device_id_type=MESH)
        return carry

    lax.fori_loop(1, 32, greet, 0)

    def three_sides(c, e):
        total = side(c, e, 0, c + 1, vg, sx) + side(c, e, 1, c, vg, sx) + side(c, e, 2, c + 2, vg, sx)
        store_blocks(total, part.at[0, e])

    def first_cell(e, carry):
        three_sides(1, e)
        return carry

    @pl.when(z == 0)
    def _():
        own.wait()
        for copy in inputs(1):
            copy.wait()
        lax.fori_loop(0, 2, first_cell, 0)

    pl.semaphore_wait(barrier, 33)

    halos = [
        pltpu.make_async_remote_copy(
            s.at[:, pl.ds(e, 1), pl.ds(source, 1)], sx.at[:, pl.ds(e, 1), pl.ds(target, 1)],
            halo_send.at[e, k], halo_recv.at[e, k], device_id=(me, where), device_id_type=MESH,
        )
        for e in range(2)
        for k, (source, target, where) in enumerate(((3, 0, up), (0, 5, down)))
    ]
    for halo in halos:
        halo.start()
    build_kernels(screened, kmat)

    @pl.when(z != 0)
    def _():
        own.wait()

    def send_energy(c, e, source):
        select(c, e, kept, count, source, sel32)
        pack(c, e, sel32, send_a)
        pltpu.make_async_copy(send_a.at[c, me, e], recv_a.at[c, me, e], a_recv.at[c]).start()

        for to in targets:
            pltpu.make_async_remote_copy(
                send_a.at[c, to, e], recv_a.at[c, me, e], a_send.at[c], a_recv.at[c],
                device_id=(to, z), device_id_type=MESH,
            ).start()

    def convolve(c):
        pltpu.make_async_copy(recv_a.at[c], recv_a.at[c], a_recv.at[c]).wait()

        def put(value):
            send_b[c] = value.reshape(32, 4, KMAX, LANES)

        conv_cell(kmat[c], lambda: recv_a[c], x32, o32, put)
        mine = pl.ds(pl.multiple_of(me * LANES, LANES), LANES)
        pltpu.make_async_copy(send_b.at[c, me], out.at[:, c, :, mine], b_recv.at[c]).start()

        for to in targets:
            pltpu.make_async_remote_copy(
                send_b.at[c, to], out.at[:, c, :, mine], b_send.at[c], b_recv.at[c],
                device_id=(to, z), device_id_type=MESH,
            ).start()

    def both(work):
        def energy(e, carry):
            work(e)
            return carry

        lax.fori_loop(0, 2, energy, 0)

    def inner_cell(i, carry):
        c = 1 + i
        fresh = jnp.logical_or(z != 0, i == 1)

        @pl.when(fresh)
        def _():
            for copy in inputs(c):
                copy.wait()

        def work(e):
            @pl.when(fresh)
            def _():
                three_sides(c, e)

            send_energy(c, e, part.at[0, e])

        both(work)
        return carry

    def edge_start(i, carry):
        c = 3 * i
        for copy in inputs(c):
            copy.wait()

        def work(e):
            store_blocks(side(c, e, 0, c + 1, vg, sx) + side(c, e, 2 - i, 2 + i, vg, sx), part.at[i, e])

        both(work)

        @pl.when(z == 7 * i)
        def _():
            both(lambda e: send_energy(c, e, part.at[i, e]))

        @pl.when(i == 0)
        def _():
            convolve(1)

        return carry

    def edge_end(e):
        def one(i, carry):
            c = 3 * i

            @pl.when(z != 7 * i)
            def _():
                total = side(c, e, 1 + i, 5 * i, vg, sx)
                for rb in range(ORB // SUB):
                    for cb in range(ORB // SUB):
                        block = total[rb * SUB : (rb + 1) * SUB, cb * LANES : (cb + 1) * LANES]
                        part[i, e, rb * 4 + cb] += block
                send_energy(c, e, part.at[i, e])

            return carry

        lax.fori_loop(0, 2, one, 0)

    lax.fori_loop(0, 2, inner_cell, 0)
    lax.fori_loop(0, 2, edge_start, 0)

    def tail(e, carry):
        for k in range(2):
            pltpu.make_async_copy(
                sx.at[:, pl.ds(e, 1), pl.ds(5 * k, 1)], sx.at[:, pl.ds(e, 1), pl.ds(5 * k, 1)], halo_recv.at[e, k]
            ).wait()
        edge_end(e)
        return carry

    lax.fori_loop(0, 2, tail, 0)

    def last_cells(i, carry):
        convolve(jnp.where(i == 0, 2, 3 * i - 3))
        return carry

    lax.fori_loop(0, 3, last_cells, 0)
    for halo in halos:
        halo.wait_send()
    for c in range(4):
        pltpu.make_async_copy(out.at[:, c], out.at[:, c], b_recv.at[c]).wait()
        sent = send_a.at[c, pl.ds(0, 31)]
        pltpu.make_async_copy(sent, sent, a_send.at[c]).wait()
        sent = send_b.at[c, pl.ds(0, 31)]
        pltpu.make_async_copy(sent, sent, b_send.at[c]).wait()


VM = pl.BlockSpec(memory_space=pltpu.VMEM)
SM = pl.BlockSpec(memory_space=pltpu.SMEM)
ANY = pl.BlockSpec(memory_space=pl.ANY)
MESH = pl.DeviceIdType.MESH


def per_device(gd, gl, gu, s, screened, kept, count):
    dma = pltpu.SemaphoreType.DMA
    out = pl.pallas_call(
        whole,
        out_shape=pltpu.VMEM((4, 4, KMAX, SUB * SUB), BF),
        in_specs=[SM, SM, VM, ANY, ANY, ANY, ANY],
        out_specs=VM,
        scratch_shapes=[
            pltpu.VMEM((3, 2, 2, 4, ORB, ORB), BF),
            pltpu.VMEM((2, 2, 6, ORB, ORB), BF),
            pltpu.VMEM((2, 2, 16, SUB, LANES), F32),
            pltpu.VMEM((16 * SUB, LANES), F32),
            pltpu.VMEM((4, 32, 2, 2, KMAX, LANES), BF),
            pltpu.VMEM((4, 32, 2, 2, KMAX, LANES), BF),
            pltpu.VMEM((4, LANES, LANES), BF),
            pltpu.VMEM((32 * 32, LANES), F32),
            pltpu.VMEM((LANES * KMAX, LANES), F32),
            pltpu.VMEM((4, 32, 4, KMAX, LANES), BF),
            dma((4, 3)),
            dma(()),
            dma((2, 2)),
            dma((2, 2)),
            dma((4,)),
            dma((4,)),
            dma((4,)),
            dma((4,)),
        ],
        compiler_params=pltpu.CompilerParams(
            vmem_limit_bytes=60 * 1024 * 1024, collective_id=0, has_side_effects=True
        ),
        name="whole",
    )(kept, count, screened, gd, gl, gu, s)
    return out.reshape(2, 2, 4, KMAX, SUB * SUB)


def solution(mesh):
    placed = P(None, "energy", "cell", None, None)
    return jax.shard_map(
        per_device,
        mesh=mesh,
        in_specs=(placed, placed, placed, placed, P(None, "cell", None), P("cell", None), P("cell")),
        out_specs=placed,
        check_vma=False,
    )
```
